256 devices in a mesh: ctx: 128 (over x, y, z_lo, core), tp: 2 (over z_hi).
Axes of the slice: x: 4, y: 4, z: 8 (z_hi: 2, z_lo: 4; z = z_hi * 4 + z_lo), core: 2. Of those that a mesh axis runs over, the one named last changes fastest.
Arguments:
- queries: bfloat16 [65536, 2048], P('ctx', 'tp'), may hold values from -7 to 7
- key_rows: bfloat16 [65536, 2048], P('ctx', 'tp'), may hold values from -7 to 7
- value_rows: bfloat16 [65536, 2048], P('ctx', 'tp'), may hold values from -6 to 6
Outputs:
- attended: bfloat16 [65536, 2048], P(('ctx', 'tp'))
The draws below stay inside these ranges and needn't reach their ends.
All inputs are finite; a program needn't handle non-finite values.
Results may differ from the reference program's by a relative error of at most 0.0029.
Values may be sent and summed in bfloat16 or wider, within the bound.
No kernel may reach another device: no remote copies, remote signals or barrier semaphores. Data moves between devices by JAX's collectives and lax.ppermute only.
A program may use at most 64 MiB of HBM per device.

```python
import math
import jax
import jax.numpy as jnp
from jax import lax

HEADS = 16
HEAD_DIM = 128
TOKENS_PER_SHARD = 512
DILATION_SECOND = 4
DILATION_THIRD = 16
DILATION_FOURTH = 64
TOKEN_COUNT = 65536


def shared_draw(key):
    base_key = jax.random.fold_in(key, 7)
    feature_count = HEADS * HEAD_DIM
    shape_pair = (TOKEN_COUNT, feature_count)
    query_draw = jnp.clip(1.5 * jax.random.normal(jax.random.fold_in(base_key, 1), shape_pair, jnp.float32), -6.0, 6.0)
    key_draw = jnp.clip(1.5 * jax.random.normal(jax.random.fold_in(base_key, 2), shape_pair, jnp.float32), -6.0, 6.0)
    return (query_draw, key_draw)


def draw_queries(key, part):
    return shared_draw(key)[0].astype(jnp.bfloat16)


def draw_key_rows(key, part):
    return shared_draw(key)[1].astype(jnp.bfloat16)


def levels(stream_key, extent, cuts, smallest, high):
    level = 1.0
    for dim, blocks in cuts:
        steps = jax.random.uniform(jax.random.fold_in(jax.random.fold_in(stream_key, 6), dim), (blocks,), jnp.float32, smallest / len(cuts), high / len(cuts))
        level = level * jnp.repeat(jnp.exp(steps), extent[dim] // blocks).reshape((-1,) + (1,) * (len(extent) - 1 - dim))
    return level


def scatter_about(stream_key, shape, spread, bound, shards=(), held_as=jnp.bfloat16):
    array = spread * jax.random.normal(stream_key, shape, jnp.float32)
    if shards:
        array = array * levels(stream_key, shape, shards, -0.22, 0.18)
    return jnp.clip(array, -bound, bound).astype(held_as)


def setup_inputs(seed: int = 0) -> dict:
    key_list = jax.random.split(jax.random.key(seed), 4)
    queries = draw_queries(jax.random.fold_in(key_list[3], 71), 0)
    key_rows = draw_key_rows(jax.random.fold_in(key_list[3], 71), 0)
    value_rows = scatter_about(key_list[2], (TOKEN_COUNT, HEADS * HEAD_DIM), 1.0, 6.0, ((0, 128), (1, 2)))
    return {"queries": queries, "key_rows": key_rows, "value_rows": value_rows}


masked_score = -1e+30

def one_segment(triple):
    query_part, key_part, value_part = triple
    seg_rows = query_part.shape[0]
    allowed = jnp.tril(jnp.ones((seg_rows, seg_rows), dtype=bool))
    scores = jnp.dot(query_part, key_part.T, preferred_element_type=jnp.float32) * (1.0 / math.sqrt(HEAD_DIM))
    scores = jnp.where(allowed, scores, masked_score)
    row_max = lax.optimization_barrier(jnp.max(scores, axis=1))
    exponent = jnp.exp(scores - row_max[:, None])
    row_sum = lax.optimization_barrier(jnp.sum(exponent, axis=1))
    weighted = jnp.dot(exponent.astype(jnp.bfloat16), value_part, preferred_element_type=jnp.float32)
    return (row_max, row_sum, weighted)

def level_terms(query_col, key_col, value_col, head_id, segment, dilation):
    selected = TOKEN_COUNT // dilation
    seg_rows = segment // dilation
    groups = TOKEN_COUNT // segment
    offset = head_id % dilation

    def pick(column):
        return column.reshape(selected, dilation, HEAD_DIM)[:, offset, :].reshape(groups, seg_rows, HEAD_DIM)
    row_max, row_sum, weighted = lax.map(one_segment, (pick(query_col), pick(key_col), pick(value_col)))
    max_full = jnp.full((selected, dilation), masked_score, jnp.float32).at[:, offset].set(row_max.reshape(selected)).reshape(TOKEN_COUNT)
    sum_full = jnp.zeros((selected, dilation), jnp.float32).at[:, offset].set(row_sum.reshape(selected)).reshape(TOKEN_COUNT)
    weighted_full = jnp.zeros((selected, dilation, HEAD_DIM), jnp.float32).at[:, offset, :].set(weighted.reshape(selected, HEAD_DIM)).reshape(TOKEN_COUNT, HEAD_DIM)
    return (max_full, sum_full, weighted_full)

def reference(queries, key_rows, value_rows):
    layout_recipe = [(TOKENS_PER_SHARD, 1), (DILATION_SECOND * TOKENS_PER_SHARD, DILATION_SECOND), (DILATION_THIRD * TOKENS_PER_SHARD, DILATION_THIRD), (TOKEN_COUNT, DILATION_FOURTH)]
    columns = []
    for head_id in range(HEADS):
        first = head_id * HEAD_DIM
        query_col = queries[:, first:first + HEAD_DIM]
        key_col = key_rows[:, first:first + HEAD_DIM]
        value_col = value_rows[:, first:first + HEAD_DIM]
        outcomes = [level_terms(query_col, key_col, value_col, head_id, segment, dilation) for segment, dilation in layout_recipe]
        peak_max = outcomes[0][0]
        for outcome in outcomes[1:]:
            peak_max = jnp.maximum(peak_max, outcome[0])
        numerator = jnp.zeros((TOKEN_COUNT, HEAD_DIM), jnp.float32)
        denominator = jnp.zeros((TOKEN_COUNT,), jnp.float32)
        for outcome in outcomes:
            factor = jnp.exp(outcome[0] - peak_max)
            numerator = numerator + factor[:, None] * outcome[2]
            denominator = denominator + factor * outcome[1]
        columns.append((numerator / denominator[:, None]).astype(jnp.bfloat16))
    return jnp.concatenate(columns, axis=1)
```

```python
import math

import jax
import jax.numpy as jnp
from jax import lax
from jax.experimental import pallas as pl
from jax.experimental.pallas import tpu as pltpu
from jax.sharding import PartitionSpec as P

F32 = jnp.float32
BF16 = jnp.bfloat16
HD = 128
NEG = -1e30
SCALE = 1.0 / math.sqrt(HD)
VMEM = pltpu.VMEM


def dot_t(a, b):
    return lax.dot_general(a, b, (((1,), (1,)), ((), ())), preferred_element_type=F32)


def dot(a, b):
    return lax.dot_general(a, b, (((1,), (0,)), ((), ())), preferred_element_type=F32)


def softmax_terms(s, v):
    m = jnp.max(s, axis=1, keepdims=True)
    e = jnp.exp(s - m)
    l = jnp.sum(e, axis=1, keepdims=True)
    return m, l, dot(e.astype(BF16), v)


def iota(shape, axis):
    return lax.broadcasted_iota(jnp.int32, shape, axis)


def pack_stats(m, l):
    lane = iota((m.shape[0], HD), 1)
    return jnp.where(lane < 64, m, l)


def select_kernel(sc, q, k, v, q1, kv1, x2, wide, mid):
    h = pl.program_id(0)
    off = 2 * sc[0] + h // 4
    far = []
    for n, ref in enumerate((q, k, v)):
        wide[...] = ref[...].astype(F32)
        rows = wide[pl.ds(h % 4, 128, stride=4), :]
        mid[...] = rows
        if n == 0:
            q1[0] = rows.astype(BF16)
        else:
            kv1[n - 1, 0] = rows.astype(BF16)
            far.append(mid[pl.ds(off, 8, stride=16), :])
        x2[0, 32 * n : 32 * n + 32] = mid[pl.ds(off, 32, stride=4), :].astype(BF16)
    x2[0, 96:112] = jnp.concatenate(far, axis=0).astype(BF16)


def local_kernel(sc, q, k, v, keep, send, part, outs, sums, stats):
    h = pl.program_id(0)
    tp = sc[0]
    for b in range(2):
        rows = pl.ds(256 * b, 256)
        width = 256 * (b + 1)
        s = dot_t(q[rows, :], k[:width, :]) * SCALE
        ok = iota(s.shape, 1) <= iota(s.shape, 0) + 256 * b
        m, l, a = softmax_terms(jnp.where(ok, s, NEG), v[:width, :])
        outs[rows, :] = a / l
        sums[rows, :] = a
        stats[rows, :] = pack_stats(m, l)
    for n in range(3):
        r = (h + n + 1) % 4
        keep[0, n] = outs[pl.ds(r + 256 * tp, 64, stride=4), :].astype(BF16)
        send[0, n] = outs[pl.ds(r + 256 * (1 - tp), 64, stride=4), :].astype(BF16)
    part[0, :, :HD] = sums[pl.ds(h % 4, 128, stride=4), :]
    part[0, :, HD:] = stats[pl.ds(h % 4, 128, stride=4), :]


def near_kernel(sc, q1, own, mate, far_a, far_b, part, keep, send, keep2, send2, outs, sums):
    h = pl.program_id(0)
    tp, c4 = sc[0], sc[1]
    keys = jnp.concatenate([far_a[0, 0], far_b[0, 0], mate[0, 0], own[0, 0]], axis=0)
    vals = jnp.concatenate([far_a[1, 0], far_b[1, 0], mate[1, 0], own[1, 0]], axis=0)
    s = dot_t(q1[0], keys) * SCALE
    row, col = iota(s.shape, 0), iota(s.shape, 1)
    start = jnp.where(c4 >= 2, 0, 256)
    stop = jnp.where(c4 % 2 == 1, 384, 256)
    ok = ((col >= start) & (col < stop)) | ((col >= 384) & (col - 384 <= row))
    m1, l1, a1 = softmax_terms(jnp.where(ok, s, NEG), vals)
    a0 = part[0, :, :HD]
    m0 = part[0, :, HD : HD + 1]
    l0 = part[0, :, HD + 64 : HD + 65]
    top = jnp.maximum(m0, m1)
    e0, e1 = jnp.exp(m0 - top), jnp.exp(m1 - top)
    num = e0 * a0 + e1 * a1
    den = e0 * l0 + e1 * l1
    outs[...] = num / den
    keep[0] = outs[pl.ds(pl.multiple_of(64 * tp, 64), 64), :].astype(BF16)
    send[0] = outs[pl.ds(pl.multiple_of(64 * (1 - tp), 64), 64), :].astype(BF16)
    sums[0] = num
    sums[1] = pack_stats(top, den)
    off = 2 * tp + h // 4
    for n in range(2):
        cols = pl.ds(HD * n, HD)
        keep2[0, :, cols] = sums[n, pl.ds(off + 64 * tp, 16, stride=4), :]
        send2[0, :, cols] = sums[n, pl.ds(off + 64 * (1 - tp), 16, stride=4), :]


def far_kernel(sc, own, mate, line, g1, g2, g3, out, rows, sums, stats):
    x, y = sc[0], sc[1]
    blk = own[...].astype(F32)
    part = [blk[:, 32 * n : 32 * n + 32].reshape(256, HD) for n in range(3)]
    q2, k2, v2 = [p.astype(BF16) for p in part]
    rows[...] = part[0]
    oth = mate[...].astype(F32)
    k2o = oth[:, 0:32].reshape(256, HD).astype(BF16)
    v2o = oth[:, 32:64].reshape(256, HD).astype(BF16)
    s = dot_t(q2, jnp.concatenate([k2o, k2], axis=0)) * SCALE
    row, col = iota(s.shape, 0), iota(s.shape, 1)
    ok = ((col < 256) & (y % 2 == 1)) | ((col >= 256) & (col - 256 <= row))
    m2, l2, a2 = softmax_terms(jnp.where(ok, s, NEG), jnp.concatenate([v2o, v2], axis=0))
    sums[...] = a2
    stats[...] = pack_stats(m2, l2)

    q3 = rows[pl.ds(0, 64, stride=4), :].astype(BF16)
    keys, vals = [], []
    for ref in (g1, g2, g3, line):
        for j in range(4):
            b = ref[j].astype(F32)
            keys.append(b[:, 0:8].reshape(64, HD))
            vals.append(b[:, 8:16].reshape(64, HD))
    keys = jnp.concatenate(keys, axis=0).astype(BF16)
    vals = jnp.concatenate(vals, axis=0).astype(BF16)
    s = dot_t(q3, keys) * SCALE
    row, col = iota(s.shape, 0), iota(s.shape, 1)
    slot = col // 64
    earlier_x = (slot < 12) & (slot // 4 + 1 <= x)
    theirs = jnp.bitwise_xor(slot - 12, y)
    earlier_y = (slot > 12) & (theirs < y)
    mine = (slot == 12) & (col - 768 <= row)
    m3, l3, a3 = softmax_terms(jnp.where(earlier_x | earlier_y | mine, s, NEG), vals)
    a2 = sums[pl.ds(0, 64, stride=4), :]
    st = stats[pl.ds(0, 64, stride=4), :]
    m2, l2 = st[:, 0:1], st[:, 64:65]
    top = jnp.maximum(m2, m3)
    e2, e3 = jnp.exp(m2 - top), jnp.exp(m3 - top)
    sums[pl.ds(0, 64, stride=4), :] = e2 * a2 + e3 * a3
    stats[pl.ds(0, 64, stride=4), :] = pack_stats(top, e2 * l2 + e3 * l3)
    for j in range(16):
        out[j, :, :HD] = sums[16 * j : 16 * j + 16, :]
        out[j, :, HD:] = stats[16 * j : 16 * j + 16, :]


def join_kernel(sc, ka, kb, k2, ra, rb, r2, back, out, wide):
    tp = sc[0]
    for side, (first, second, third) in enumerate(((ka, kb, k2), (ra, rb, r2))):
        src = tp if side == 0 else 1 - tp
        for h in range(8):
            for n in range(3):
                wide[pl.ds((h + n + 1) % 4, 64, stride=4), :] = first[h, n].astype(F32)
            wide[pl.ds(h % 4, 64, stride=4), :] = second[h].astype(F32)
            mine = third[h]
            a0, m0, l0 = mine[:, :HD], mine[:, HD : HD + 1], mine[:, HD + 64 : HD + 65]
            more = back[2 * h + src]
            a1, m1, l1 = more[:, :HD], more[:, HD : HD + 1], more[:, HD + 64 : HD + 65]
            top = jnp.maximum(m0, m1)
            e0, e1 = jnp.exp(m0 - top), jnp.exp(m1 - top)
            wide[pl.ds(8 * src + h, 16, stride=16), :] = (e0 * a0 + e1 * a1) / (e0 * l0 + e1 * l1)
            cols = pl.ds(pl.multiple_of(src * 1024 + h * HD, HD), HD)
            out[:, cols] = wide[...].astype(BF16)


def spec(shape, index):
    return pl.BlockSpec(shape, index)


def head_call(kernel, name, ins, in_specs, outs, out_specs, scratch, scalars):
    return pl.pallas_call(
        kernel,
        out_shape=outs,
        grid_spec=pltpu.PrefetchScalarGridSpec(
            num_scalar_prefetch=1,
            grid=(8,),
            in_specs=in_specs,
            out_specs=out_specs,
            scratch_shapes=scratch,
        ),
        name=name,
    )(scalars, *ins)


def shape(dims, dtype):
    return jax.ShapeDtypeStruct(dims, dtype)


def local(queries, key_rows, value_rows):
    c = lax.axis_index("ctx")
    tp = lax.axis_index("tp")
    tps = jnp.stack([tp, c % 4]).astype(jnp.int32)
    xys = jnp.stack([c // 32, (c // 8) % 4]).astype(jnp.int32)

    cols = spec((512, HD), lambda h, s: (0, h))
    q1, kv1, x2 = head_call(
        select_kernel, "select", (queries, key_rows, value_rows), [cols] * 3,
        (shape((8, 128, HD), BF16), shape((2, 8, 128, HD), BF16), shape((8, 112, HD), BF16)),
        (spec((1, 128, HD), lambda h, s: (h, 0, 0)),
         spec((2, 1, 128, HD), lambda h, s: (0, h, 0, 0)),
         spec((1, 112, HD), lambda h, s: (h, 0, 0))),
        [VMEM((512, HD), F32), VMEM((128, HD), F32)], tps)

    n = 128
    mate = lax.ppermute(kv1, "ctx", [(i, i + 1) for i in range(0, n, 2)])
    far_a = lax.ppermute(kv1, "ctx", [(i, i + 2) for i in range(n) if i % 4 < 2])

    groups = [[8 * b + i for i in range(8)] for b in range(16)]
    y2 = lax.all_to_all(
        x2, "ctx", split_axis=0, concat_axis=0, tiled=True, axis_index_groups=groups)

    kv2 = y2[:, 32:112]
    kv3 = y2[:, 96:112]

    def flip_y(value, k):
        return lax.ppermute(value, "ctx", [(i, i ^ (8 * k)) for i in range(n)])

    from_1 = flip_y(kv2, 1)
    from_2 = flip_y(kv3, 2)
    from_3 = flip_y(kv3, 3)
    line = jnp.stack([kv3, from_1[:, 64:80], from_2, from_3])
    ahead = [
        lax.ppermute(line, "ctx", [(i, i + 32 * d) for i in range(n - 32 * d)]) for d in (1, 2, 3)
    ]
    far_b = lax.ppermute(far_a, "ctx", [(i, i ^ 1) for i in range(n) if i % 4 >= 2])

    rows3 = spec((1, 3, 64, HD), lambda h, s: (h, 0, 0, 0))
    keep, send, part = head_call(
        local_kernel, "local", (queries, key_rows, value_rows), [cols] * 3,
        (shape((8, 3, 64, HD), BF16), shape((8, 3, 64, HD), BF16), shape((8, 128, 256), F32)),
        (rows3, rows3, spec((1, 128, 256), lambda h, s: (h, 0, 0))),
        [VMEM((512, HD), F32)] * 3, tps)
    swap = [(0, 1), (1, 0)]
    got = lax.ppermute(send, "tp", swap)

    pair = spec((2, 1, 128, HD), lambda h, s: (0, h, 0, 0))
    half = spec((1, 64, HD), lambda h, s: (h, 0, 0))
    few = spec((1, 16, 256), lambda h, s: (h, 0, 0))
    keep1, send1, keep2, send2 = head_call(
        near_kernel, "near", (q1, kv1, mate, far_a, far_b, part),
        [spec((1, 128, HD), lambda h, s: (h, 0, 0)), pair, pair, pair, pair,
         spec((1, 128, 256), lambda h, s: (h, 0, 0))],
        (shape((8, 64, HD), BF16), shape((8, 64, HD), BF16),
         shape((8, 16, 256), F32), shape((8, 16, 256), F32)),
        (half, half, few, few),
        [VMEM((128, HD), F32), VMEM((2, 128, HD), F32)], tps)
    got1 = lax.ppermute(send1, "tp", swap)
    got2 = lax.ppermute(send2, "tp", swap)

    smem = pl.BlockSpec(memory_space=pltpu.SMEM)
    vm = pl.BlockSpec(memory_space=pltpu.VMEM)
    back = pl.pallas_call(
        far_kernel,
        out_shape=shape((16, 16, 256), F32),
        in_specs=[smem] + [vm] * 6,
        out_specs=vm,
        scratch_shapes=[VMEM((256, HD), F32)] * 3,
        name="far",
    )(xys, y2, from_1, line, *ahead)
    groups2 = [[16 * b + i for i in range(16)] for b in range(16)]
    back = lax.all_to_all(
        back, ("ctx", "tp"), split_axis=0, concat_axis=0, tiled=True, axis_index_groups=groups2)

    return pl.pallas_call(
        join_kernel,
        out_shape=shape((256, 2048), BF16),
        in_specs=[smem] + [vm] * 7,
        out_specs=vm,
        scratch_shapes=[VMEM((256, HD), F32)],
        name="join",
    )(tps, keep, keep1, keep2, got, got1, got2, back)


def solution(mesh):
    return jax.shard_map(
        local,
        mesh=mesh,
        in_specs=(P("ctx", "tp"), P("ctx", "tp"), P("ctx", "tp")),
        out_specs=P(("ctx", "tp"), None),
        check_vma=False,
    )
```

```python
import math

import jax
import jax.numpy as jnp
from jax import lax
from jax.experimental import pallas as pl
from jax.experimental.pallas import tpu as pltpu
from jax.sharding import PartitionSpec as P

F32 = jnp.float32
BF16 = jnp.bfloat16
HD = 128
NEG = -1e30
SCALE = math.log2(math.e) / math.sqrt(HD)
VMEM = pltpu.VMEM
LIMIT = 24 * 2**20


def dot_t(a, b):
    return lax.dot_general(a, b, (((1,), (1,)), ((), ())), preferred_element_type=F32)


def dot(a, b):
    return lax.dot_general(a, b, (((1,), (0,)), ((), ())), preferred_element_type=F32)


def iota(shape, axis):
    return lax.broadcasted_iota(jnp.int32, shape, axis)


def attend(s, v):
    m = jnp.max(s, axis=1, keepdims=True)
    e = jnp.exp2(s - m)
    l = jnp.sum(e, axis=1, keepdims=True)
    return dot(e.astype(BF16), v) / l, m + jnp.log2(l)


def merge(o0, z0, o1, z1):
    top = jnp.maximum(z0, z1)
    w0, w1 = jnp.exp2(z0 - top), jnp.exp2(z1 - top)
    den = w0 + w1
    return (w0 * o0 + w1 * o1) / den, top + jnp.log2(den)


def split3(z):
    hi = z.astype(BF16).astype(F32)
    mid = (z - hi).astype(BF16).astype(F32)
    lo = z - hi - mid
    lane = iota((z.shape[0], HD), 1)
    out = jnp.where(lane == 0, hi, jnp.where(lane == 1, mid, jnp.where(lane == 2, lo, 0.0)))
    return out.astype(BF16)


def join3(p):
    return jnp.sum(p.astype(F32), axis=1, keepdims=True)


def head(h):
    return slice(h * HD, (h + 1) * HD)


def head_copies(hbm, vmem, sems):
    def copy(n, h):
        return pltpu.make_async_copy(
            hbm[n].at[:, head(h)], vmem.at[n, :, head(h)], sems.at[n, h])

    for h in range(8):
        for n in range(3):
            copy(n, h).start()

    def arrive(h):
        for n in range(3):
            copy(n, h).wait()

    return arrive


def select_kernel(q, k, v, q1, kv1, x2, rows_in, wide, s1, s2, sems, sems_out):
    tp = lax.axis_index("tp")
    arrive = head_copies((q, k, v), rows_in, sems)
    pending = []

    def leave(src, dst, slot, h):
        copy = pltpu.make_async_copy(src, dst, sems_out.at[slot, h])
        copy.start()
        pending.append(copy)

    for h in range(8):
        arrive(h)
        far = []
        for n in range(3):
            buf = wide.at[(3 * h + n) % 6]
            buf[...] = rows_in[n, :, head(h)].astype(F32)
            s1[n, h] = buf[pl.ds(h % 4, 128, stride=4), :].astype(BF16)
            if n > 0:
                far.append(buf[pl.ds(8 * tp + h, 8, stride=64), :])
            s2[h, 32 * n : 32 * n + 32] = buf[pl.ds(8 * tp + h, 32, stride=16), :].astype(BF16)
        s2[h, 96:112] = jnp.concatenate(far, axis=0).astype(BF16)
        leave(s2.at[h], x2.at[h], 0, h)
        leave(s1.at[0, h], q1.at[h], 1, h)
        leave(s1.at[1, h], kv1.at[0, h], 2, h)
        leave(s1.at[2, h], kv1.at[1, h], 3, h)
    for copy in pending:
        copy.wait()


def local_kernel(q, k, v, keep, send, part, rows_in, mine, theirs, outs, stats, sems, sems_out):
    tp = lax.axis_index("tp")
    arrive = head_copies((q, k, v), rows_in, sems)
    pending = []
    ok = iota((256, 256), 1) <= iota((256, 256), 0)
    for h in range(8):
        arrive(h)
        o_ref, z_ref = outs.at[h % 4], stats.at[h % 4]
        for b in range(2):
            rows = slice(256 * b, 256 * b + 256)
            upto = slice(0, 256 * b + 256)
            s = dot_t(rows_in[0, rows, head(h)], rows_in[1, upto, head(h)]) * SCALE
            last = jnp.where(ok, s[:, 256 * b :], NEG)
            s = last if b == 0 else jnp.concatenate([s[:, :256], last], axis=1)
            o, z = attend(s, rows_in[2, upto, head(h)])
            o_ref[rows, :] = o
            z_ref[rows, :] = jnp.broadcast_to(z, (256, HD))
        for n in range(3):
            r = (h + n + 1) % 4
            mine[h, n] = o_ref[pl.ds(r + 256 * tp, 64, stride=4), :].astype(BF16)
            theirs[h, n] = o_ref[pl.ds(r + 256 * (1 - tp), 64, stride=4), :].astype(BF16)
        for slot, (src, dst) in enumerate(((theirs, send), (mine, keep))):
            copy = pltpu.make_async_copy(src.at[h], dst.at[h], sems_out.at[slot, h])
            copy.start()
            pending.append(copy)
        part[h, :, :HD] = o_ref[pl.ds(h % 4, 128, stride=4), :]
        part[h, :, HD:] = z_ref[pl.ds(h % 4, 128, stride=4), :]
    for copy in pending:
        copy.wait()


def near_kernel(q1, own, mate, far_a, far_b, part, keep, send, outs, stats):
    tp = lax.axis_index("tp")
    c4 = lax.rem(lax.axis_index("ctx"), 4)
    row, col = iota((128, 512), 0), iota((128, 512), 1)
    start = jnp.where(c4 >= 2, 0, 256)
    stop = jnp.where(lax.rem(c4, 2) == 1, 384, 256)
    ok = ((col >= start) & (col < stop)) | ((col >= 384) & (col - 384 <= row))
    for h in range(8):
        o_ref, z_ref = outs.at[h % 4], stats.at[h % 4]
        keys = jnp.concatenate([far_a[0, h], far_b[0, h], mate[0, h], own[0, h]], axis=0)
        vals = jnp.concatenate([far_a[1, h], far_b[1, h], mate[1, h], own[1, h]], axis=0)
        s = dot_t(q1[h], keys) * SCALE
        o1, z1 = attend(jnp.where(ok, s, NEG), vals)
        o, z = merge(part[h, :, :HD], part[h, :, HD : HD + 1], o1, z1)
        o_ref[...] = o
        z_ref[...] = jnp.broadcast_to(z, (128, HD))
        for ref, side in ((keep, tp), (send, 1 - tp)):
            base = pl.multiple_of(64 * side, 64)
            ref[h, :64] = o_ref[pl.ds(base, 64), :].astype(BF16)
            few = z_ref[pl.ds(64 * side + 2 * tp + h // 4, 16, stride=4), :]
            ref[h, 64:80] = split3(few[:, 0:1])


def far_kernel(own, mate, line, g1, g2, g3, out, rows, sums, stats):
    c = lax.axis_index("ctx")
    x, y = lax.div(c, 32), lax.rem(lax.div(c, 8), 4)

    def part(ref, start):
        return ref[:, start : start + 32].astype(F32).reshape(256, HD)

    rows[...] = part(own, 0)
    keys = jnp.concatenate([part(mate, 0), part(own, 32)], axis=0).astype(BF16)
    vals = jnp.concatenate([part(mate, 32), part(own, 64)], axis=0).astype(BF16)
    s = dot_t(rows[...].astype(BF16), keys) * SCALE
    row, col = iota(s.shape, 0), iota(s.shape, 1)
    ok = ((col < 256) & (lax.rem(y, 2) == 1)) | ((col >= 256) & (col - 256 <= row))
    o2, z2 = attend(jnp.where(ok, s, NEG), vals)
    sums[...] = o2
    stats[...] = jnp.broadcast_to(z2, (256, HD))

    q3 = rows[pl.ds(0, 64, stride=4), :].astype(BF16)
    keys, vals = [], []
    for ref in (g1, g2, g3, line):
        for j in range(4):
            b = ref[j].astype(F32)
            keys.append(b[:, 0:8].reshape(64, HD))
            vals.append(b[:, 8:16].reshape(64, HD))
    keys = jnp.concatenate(keys, axis=0).astype(BF16)
    vals = jnp.concatenate(vals, axis=0).astype(BF16)
    s = dot_t(q3, keys) * SCALE
    row, col = iota(s.shape, 0), iota(s.shape, 1)
    slot = lax.shift_right_logical(col, 6)
    earlier_x = (slot < 12) & (jnp.bitwise_xor(lax.shift_right_logical(slot, 2) + 1, x) < x)
    earlier_y = (slot > 12) & (jnp.bitwise_xor(slot - 12, y) < y)
    mine = (slot == 12) & (col - 768 <= row)
    o3, z3 = attend(jnp.where(earlier_x | earlier_y | mine, s, NEG), vals)
    pick = pl.ds(0, 64, stride=4)
    o, z = merge(sums[pick, :], stats[pick, :][:, 0:1], o3, z3)
    sums[pick, :] = o
    stats[pick, :] = jnp.broadcast_to(z, (64, HD))
    for j in range(16):
        out[j, :, :HD] = sums[16 * j : 16 * j + 16, :].astype(BF16)
        out[j, :, HD:] = split3(stats[16 * j : 16 * j + 16, :][:, 0:1])


def join_kernel(ka, kb, ra, rb, back, out, wide):
    tp = lax.axis_index("tp")
    for h in range(8):
        for side, (first, second) in enumerate(((ka, kb), (ra, rb))):
            src = tp if side == 0 else 1 - tp
            buf = wide.at[(2 * h + side) % 4]
            for n in range(3):
                buf[pl.ds((h + n + 1) % 4, 64, stride=4), :] = first[h, n].astype(F32)
            buf[pl.ds(h % 4, 64, stride=4), :] = second[h, :64].astype(F32)
            pick = pl.ds(8 * src + h, 16, stride=16)
            more = back[2 * h + src]
            o, _ = merge(
                buf[pick, :], join3(second[h, 64:80]), more[:, :HD].astype(F32), join3(more[:, HD:]))
            buf[pick, :] = o
            cols = pl.ds(pl.multiple_of(src * 1024 + h * HD, HD), HD)
            out[:, cols] = buf[...].astype(BF16)


def call(kernel, name, ins, outs, scratch):
    vm, hbm = pl.BlockSpec(memory_space=VMEM), pl.BlockSpec(memory_space=pltpu.HBM)
    spaces = {"V": VMEM, "H": pltpu.HBM}
    args = [pltpu.with_memory_space_constraint(a, spaces[m]) if m else a for a, m in ins]
    return pl.pallas_call(
        kernel,
        out_shape=[spaces[m](*o) if m else jax.ShapeDtypeStruct(*o) for o, m in outs],
        in_specs=[hbm if m == "H" else vm for _, m in ins],
        out_specs=[hbm if m == "H" else vm for _, m in outs],
        scratch_shapes=scratch,
        compiler_params=pltpu.CompilerParams(vmem_limit_bytes=LIMIT),
        name=name,
    )(*args)


def local(queries, key_rows, value_rows):
    n = 128

    def exchange(value, axes, size, total):
        groups = [[size * b + i for i in range(size)] for b in range(total // size)]
        return lax.all_to_all(
            value, axes, split_axis=0, concat_axis=0, tiled=True, axis_index_groups=groups)

    def flip(value, bits):
        return lax.ppermute(value, "ctx", [(i, i ^ bits) for i in range(n)])

    barrier = lax.optimization_barrier
    dma = pltpu.SemaphoreType.DMA
    args = [(queries, "H"), (key_rows, "H"), (value_rows, "H")]
    q1, kv1, x2 = call(
        select_kernel, "select", args,
        ((((8, 128, HD), BF16), "H"), (((2, 8, 128, HD), BF16), "H"), (((8, 112, HD), BF16), "H")),
        [VMEM((3, 512, 1024), BF16), VMEM((6, 512, HD), F32), VMEM((3, 8, 128, HD), BF16),
         VMEM((8, 112, HD), BF16), dma((3, 8)), dma((4, 8))])
    y2 = exchange(x2, "ctx", 8, n)
    mate = flip(kv1, 1)
    far_a = flip(kv1, 2)

    y2, queries, key_rows, value_rows = barrier((y2, queries, key_rows, value_rows))
    kv2 = y2[:, 32:112]
    kv3 = y2[:, 96:112]
    flips = [flip(kv2 if j == 1 else kv3, 8 * j) for j in (1, 2, 3)]

    keep, send, part = call(
        local_kernel, "local", [(queries, "H"), (key_rows, "H"), (value_rows, "H")],
        ((((8, 3, 64, HD), BF16), "H"), (((8, 3, 64, HD), BF16), "H"), (((8, 128, 256), F32), "V")),
        [VMEM((3, 512, 1024), BF16), VMEM((8, 3, 64, HD), BF16), VMEM((8, 3, 64, HD), BF16),
         VMEM((4, 512, HD), F32), VMEM((4, 512, HD), F32), dma((3, 8)), dma((2, 8))])
    swap = [(0, 1), (1, 0)]
    got = lax.ppermute(send, "tp", swap)

    line = jnp.stack([kv3, flips[0][:, 64:80], flips[1], flips[2]])
    line, far_a, part = barrier((line, far_a, part))
    ahead = [flip(line, 32 * j) for j in (1, 2, 3)]
    far_b = flip(far_a, 1)

    keep1, send1 = call(
        near_kernel, "near", [(a, "V") for a in (q1, kv1, mate, far_a, far_b, part)],
        ((((8, 80, HD), BF16), None), (((8, 80, HD), BF16), None)),
        [VMEM((4, 128, HD), F32), VMEM((4, 128, HD), F32)])
    got1 = lax.ppermute(send1, "tp", swap)

    y2, keep1 = barrier((y2, keep1))
    (back,) = call(
        far_kernel, "far", [(a, "V") for a in (y2, flips[0], line, *ahead)],
        ((((16, 16, 256), BF16), None),), [VMEM((256, HD), F32)] * 3)
    back = exchange(back, ("ctx", "tp"), 16, 2 * n)

    (out,) = call(
        join_kernel, "join", [(a, "V") for a in (keep, keep1, got, got1, back)],
        ((((256, 2048), BF16), None),), [VMEM((4, 256, HD), F32)])
    return out


def solution(mesh):
    return jax.shard_map(
        local,
        mesh=mesh,
        in_specs=(P("ctx", "tp"), P("ctx", "tp"), P("ctx", "tp")),
        out_specs=P(("ctx", "tp"), None),
        check_vma=False,
    )
```

```python
import math

import jax
import jax.numpy as jnp
from jax import lax
from jax.experimental import pallas as pl
from jax.experimental.pallas import tpu as pltpu
from jax.sharding import PartitionSpec as P


F32 = jnp.float32
BF16 = jnp.bfloat16
HD = 128
NEG = -1e30
SCALE = math.log2(math.e) / math.sqrt(HD)
VMEM = pltpu.VMEM
LIMIT = 24 * 2**20


def dot_t(a, b):
    return lax.dot_general(a, b, (((1,), (1,)), ((), ())), preferred_element_type=F32)


def dot(a, b):
    return lax.dot_general(a, b, (((1,), (0,)), ((), ())), preferred_element_type=F32)


def iota(shape, axis):
    return lax.broadcasted_iota(jnp.int32, shape, axis)


def attend(s, v):
    m = jnp.max(s, axis=1, keepdims=True)
    e = jnp.exp2(s - m)
    l = jnp.sum(e, axis=1, keepdims=True)
    return dot(e.astype(BF16), v) / l, m + jnp.log2(l)


def merge(o0, z0, o1, z1):
    top = jnp.maximum(z0, z1)
    w0, w1 = jnp.exp2(z0 - top), jnp.exp2(z1 - top)
    den = w0 + w1
    return (w0 * o0 + w1 * o1) / den, top + jnp.log2(den)


def split3(z):
    hi = z.astype(BF16).astype(F32)
    mid = (z - hi).astype(BF16).astype(F32)
    lo = z - hi - mid
    lane = iota((z.shape[0], HD), 1)
    out = jnp.where(lane == 0, hi, jnp.where(lane == 1, mid, jnp.where(lane == 2, lo, 0.0)))
    return out.astype(BF16)


def join3(p):
    return jnp.sum(p.astype(F32), axis=1, keepdims=True)


def head(h):
    return slice(h * HD, (h + 1) * HD)


def head_copies(hbm, vmem, sems):
    def copy(n, h):
        return pltpu.make_async_copy(
            hbm[n].at[:, head(h)], vmem.at[n, :, head(h)], sems.at[n, h])

    for h in range(8):
        for n in range(3):
            copy(n, h).start()

    def arrive(h):
        for n in range(3):
            copy(n, h).wait()

    return arrive


def select_kernel(q, k, v, q1, kv1, x2, rows_in, wide, s1, s2, sems, sems_out):
    tp = lax.axis_index("tp")
    arrive = head_copies((q, k, v), rows_in, sems)
    pending = []

    def leave(src, dst, slot, h):
        copy = pltpu.make_async_copy(src, dst, sems_out.at[slot, h])
        copy.start()
        pending.append(copy)

    for h in range(8):
        arrive(h)
        far = []
        for n in range(3):
            buf = wide.at[(3 * h + n) % 6]
            buf[...] = rows_in[n, :, head(h)].astype(F32)
            s1[n, h] = buf[pl.ds(h % 4, 128, stride=4), :].astype(BF16)
            if n > 0:
                far.append(buf[pl.ds(8 * tp + h, 8, stride=64), :])
            s2[h, 32 * n : 32 * n + 32] = buf[pl.ds(8 * tp + h, 32, stride=16), :].astype(BF16)
        s2[h, 96:112] = jnp.concatenate(far, axis=0).astype(BF16)
        leave(s2.at[h], x2.at[h], 0, h)
        leave(s1.at[0, h], q1.at[h], 1, h)
        leave(s1.at[1, h], kv1.at[0, h], 2, h)
        leave(s1.at[2, h], kv1.at[1, h], 3, h)
    for copy in pending:
        copy.wait()


def local_kernel(q, k, v, keep, send, part, mine, theirs, rest, outs, stats, sems_out):
    tp = lax.axis_index("tp")
    pending = []
    ok = iota((256, 256), 1) <= iota((256, 256), 0)
    for h in range(8):
        o_ref, z_ref = outs.at[h % 4], stats.at[h % 4]
        for b in range(2):
            rows = slice(256 * b, 256 * b + 256)
            upto = slice(0, 256 * b + 256)
            s = dot_t(q[rows, head(h)], k[upto, head(h)]) * SCALE
            last = jnp.where(ok, s[:, 256 * b :], NEG)
            s = last if b == 0 else jnp.concatenate([s[:, :256], last], axis=1)
            o, z = attend(s, v[upto, head(h)])
            o_ref[rows, :] = o
            z_ref[rows, :] = jnp.broadcast_to(z, (256, HD))
        for n in range(3):
            r = (h + n + 1) % 4
            mine[h, n] = o_ref[pl.ds(r + 256 * tp, 64, stride=4), :].astype(BF16)
            theirs[h, n] = o_ref[pl.ds(r + 256 * (1 - tp), 64, stride=4), :].astype(BF16)
        rest[h, :, :HD] = o_ref[pl.ds(h % 4, 128, stride=4), :]
        rest[h, :, HD:] = z_ref[pl.ds(h % 4, 128, stride=4), :]
        for slot, (src, dst) in enumerate(((theirs, send), (mine, keep), (rest, part))):
            copy = pltpu.make_async_copy(src.at[h], dst.at[h], sems_out.at[slot, h])
            copy.start()
            pending.append(copy)
    for copy in pending:
        copy.wait()


def near_kernel(
    q1_in, own_in, part_in, mate, far_a, far_b, keep, send, q1, own, part, outs, stats, sems):
    copies = [
        pltpu.make_async_copy(*pair, sems.at[n])
        for n, pair in enumerate(((q1_in, q1), (own_in, own), (part_in, part)))
    ]
    for copy in copies:
        copy.start()
    tp = lax.axis_index("tp")
    c4 = lax.rem(lax.axis_index("ctx"), 4)
    row, col = iota((128, 512), 0), iota((128, 512), 1)
    start = jnp.where(c4 >= 2, 0, 256)
    stop = jnp.where(lax.rem(c4, 2) == 1, 384, 256)
    ok = ((col >= start) & (col < stop)) | ((col >= 384) & (col - 384 <= row))
    copies[0].wait()
    copies[1].wait()
    for h in range(8):
        keys = jnp.concatenate([far_a[0, h], far_b[0, h], mate[0, h], own[0, h]], axis=0)
        vals = jnp.concatenate([far_a[1, h], far_b[1, h], mate[1, h], own[1, h]], axis=0)
        s = dot_t(q1[h], keys) * SCALE
        o, z = attend(jnp.where(ok, s, NEG), vals)
        outs[h] = o
        stats[h] = jnp.broadcast_to(z, (128, HD))
    copies[2].wait()
    for h in range(8):
        o_ref, z_ref = outs.at[h], stats.at[h]
        o, z = merge(part[h, :, :HD], part[h, :, HD:], o_ref[...], z_ref[...])
        o_ref[...] = o
        z_ref[...] = z
        for ref, side in ((keep, tp), (send, 1 - tp)):
            base = pl.multiple_of(64 * side, 64)
            ref[h, :64] = o_ref[pl.ds(base, 64), :].astype(BF16)
            few = z_ref[pl.ds(64 * side + 2 * tp + h // 4, 16, stride=4), :]
            ref[h, 64:80] = split3(few)


def far_kernel(own, mate, line, g1, g2, g3, out, rows, sums, stats):
    c = lax.axis_index("ctx")
    x, y = lax.div(c, 32), lax.rem(lax.div(c, 8), 4)

    def part(ref, start):
        return ref[:, start : start + 32].astype(F32).reshape(256, HD)

    rows[...] = part(own, 0)
    keys = jnp.concatenate([part(mate, 0), part(own, 32)], axis=0).astype(BF16)
    vals = jnp.concatenate([part(mate, 32), part(own, 64)], axis=0).astype(BF16)
    s = dot_t(rows[...].astype(BF16), keys) * SCALE
    row, col = iota(s.shape, 0), iota(s.shape, 1)
    ok = ((col < 256) & (lax.rem(y, 2) == 1)) | ((col >= 256) & (col - 256 <= row))
    o2, z2 = attend(jnp.where(ok, s, NEG), vals)
    sums[...] = o2
    stats[...] = jnp.broadcast_to(z2, (256, HD))

    q3 = rows[pl.ds(0, 64, stride=4), :].astype(BF16)
    keys, vals = [], []
    for ref in (g1, g2, g3, line):
        for j in range(4):
            b = ref[j].astype(F32)
            keys.append(b[:, 0:8].reshape(64, HD))
            vals.append(b[:, 8:16].reshape(64, HD))
    keys = jnp.concatenate(keys, axis=0).astype(BF16)
    vals = jnp.concatenate(vals, axis=0).astype(BF16)
    s = dot_t(q3, keys) * SCALE
    row, col = iota(s.shape, 0), iota(s.shape, 1)
    slot = lax.shift_right_logical(col, 6)
    earlier_x = (slot < 12) & (jnp.bitwise_xor(lax.shift_right_logical(slot, 2) + 1, x) < x)
    earlier_y = (slot > 12) & (jnp.bitwise_xor(slot - 12, y) < y)
    mine = (slot == 12) & (col - 768 <= row)
    o3, z3 = attend(jnp.where(earlier_x | earlier_y | mine, s, NEG), vals)
    pick = pl.ds(0, 64, stride=4)
    o, z = merge(sums[pick, :], stats[pick, :][:, 0:1], o3, z3)
    sums[pick, :] = o
    stats[pick, :] = jnp.broadcast_to(z, (64, HD))
    for j in range(16):
        out[j, :, :HD] = sums[16 * j : 16 * j + 16, :].astype(BF16)
        out[j, :, HD:] = split3(stats[16 * j : 16 * j + 16, :][:, 0:1])


def join_kernel(ka, kb, ra, rb, back, out, wide):
    tp = lax.axis_index("tp")
    for h in range(8):
        for side, (first, second) in enumerate(((ka, kb), (ra, rb))):
            src = tp if side == 0 else 1 - tp
            buf = wide.at[(2 * h + side) % 4]
            for n in range(3):
                buf[pl.ds((h + n + 1) % 4, 64, stride=4), :] = first[h, n].astype(F32)
            buf[pl.ds(h % 4, 64, stride=4), :] = second[h, :64].astype(F32)
            pick = pl.ds(8 * src + h, 16, stride=16)
            more = back[2 * h + src]
            o, _ = merge(
                buf[pick, :], join3(second[h, 64:80]), more[:, :HD].astype(F32), join3(more[:, HD:]))
            buf[pick, :] = o
            cols = pl.ds(pl.multiple_of(src * 1024 + h * HD, HD), HD)
            out[:, cols] = buf[...].astype(BF16)


def call(kernel, ins, outs, scratch):
    vm, hbm = pl.BlockSpec(memory_space=VMEM), pl.BlockSpec(memory_space=pltpu.HBM)
    spaces = {"V": VMEM, "H": pltpu.HBM}
    args = [pltpu.with_memory_space_constraint(a, spaces[m]) if m else a for a, m in ins]
    return pl.pallas_call(
        kernel,
        out_shape=[spaces[m](*o) if m else jax.ShapeDtypeStruct(*o) for o, m in outs],
        in_specs=[hbm if m == "H" else vm for _, m in ins],
        out_specs=[hbm if m == "H" else vm for _, m in outs],
        scratch_shapes=scratch,
        compiler_params=pltpu.CompilerParams(vmem_limit_bytes=LIMIT),
    )(*args)


def local(queries, key_rows, value_rows):
    n = 128

    def exchange(value, axes, size, total):
        groups = [[size * b + i for i in range(size)] for b in range(total // size)]
        return lax.all_to_all(
            value, axes, split_axis=0, concat_axis=0, tiled=True, axis_index_groups=groups)

    def flip(value, bits):
        return lax.ppermute(value, "ctx", [(i, i ^ bits) for i in range(n)])

    barrier = lax.optimization_barrier
    dma = pltpu.SemaphoreType.DMA
    args = [(queries, "H"), (key_rows, "H"), (value_rows, "H")]
    q1, kv1, x2 = call(
        select_kernel, args,
        ((((8, 128, HD), BF16), "H"), (((2, 8, 128, HD), BF16), "H"), (((8, 112, HD), BF16), "H")),
        [VMEM((3, 512, 1024), BF16), VMEM((6, 512, HD), F32), VMEM((3, 8, 128, HD), BF16),
         VMEM((8, 112, HD), BF16), dma((3, 8)), dma((4, 8))])
    y2 = exchange(x2, "ctx", 8, n)
    far_a = lax.ppermute(kv1, "ctx", [(i, i + 2) for i in range(n) if i % 4 < 2])
    mate = flip(kv1, 1)

    keep, send, part = call(
        local_kernel, [(a, "V") for a in (queries, key_rows, value_rows)],
        ((((8, 3, 64, HD), BF16), "H"), (((8, 3, 64, HD), BF16), "H"), (((8, 128, 256), F32), "H")),
        [VMEM((8, 3, 64, HD), BF16), VMEM((8, 3, 64, HD), BF16), VMEM((8, 128, 256), F32),
         VMEM((4, 512, HD), F32), VMEM((4, 512, HD), F32), dma((3, 8))])
    swap = [(0, 1), (1, 0)]
    y2, part = barrier((y2, part))
    kv2 = y2[:, 32:112]
    kv3 = y2[:, 96:112]
    flips = [flip(kv2 if j == 1 else kv3, 8 * j) for j in (1, 2, 3)]
    got = lax.ppermute(send, "tp", swap)

    line = jnp.stack([kv3, flips[0][:, 64:80], flips[1], flips[2]])
    ahead = [flip(line, 32 * j) for j in (1, 2, 3)]
    far_b = flip(far_a, 1)

    keep1, send1 = call(
        near_kernel,
        [(a, "H") for a in (q1, kv1, part)] + [(a, "V") for a in (mate, far_a, far_b)],
        ((((8, 80, HD), BF16), None), (((8, 80, HD), BF16), None)),
        [VMEM((8, 128, HD), BF16), VMEM((2, 8, 128, HD), BF16), VMEM((8, 128, 256), F32),
         VMEM((8, 128, HD), F32), VMEM((8, 128, HD), F32), dma((3,))])
    got1 = lax.ppermute(send1, "tp", swap)

    y2, keep1 = barrier((y2, keep1))
    (back,) = call(
        far_kernel, [(a, "V") for a in (y2, flips[0], line, *ahead)],
        ((((16, 16, 256), BF16), None),), [VMEM((256, HD), F32)] * 3)
    back = exchange(back, ("ctx", "tp"), 16, 2 * n)

    (out,) = call(
        join_kernel, [(a, "V") for a in (keep, keep1, got, got1, back)],
        ((((256, 2048), BF16), None),), [VMEM((4, 256, HD), F32)])
    return out


def solution(mesh):
    return jax.shard_map(
        local,
        mesh=mesh,
        in_specs=(P("ctx", "tp"), P("ctx", "tp"), P("ctx", "tp")),
        out_specs=P(("ctx", "tp"), None),
        check_vma=False,
    )
```

```python
import math

import jax
import jax.numpy as jnp
from jax import lax
from jax.experimental import pallas as pl
from jax.experimental.pallas import tpu as pltpu
from jax.sharding import PartitionSpec as P


F32 = jnp.float32
BF16 = jnp.bfloat16
HD = 128
NEG = -1e30
SCALE = math.log2(math.e) / math.sqrt(HD)
VMEM = pltpu.VMEM
LIMIT = 24 * 2**20


def dot_t(a, b):
    return lax.dot_general(a, b, (((1,), (1,)), ((), ())), preferred_element_type=F32)


def dot(a, b):
    return lax.dot_general(a, b, (((1,), (0,)), ((), ())), preferred_element_type=F32)


def iota(shape, axis):
    return lax.broadcasted_iota(jnp.int32, shape, axis)


def attend(s, v):
    m = jnp.max(s, axis=1, keepdims=True)
    e = jnp.exp2(s - m)
    return m, jnp.sum(e, axis=1, keepdims=True), dot(e.astype(BF16), v)


def merge(m0, l0, a0, m1, l1, a1):
    top = jnp.maximum(m0, m1)
    w0, w1 = jnp.exp2(m0 - top), jnp.exp2(m1 - top)
    return top, w0 * l0 + w1 * l1, w0 * a0 + w1 * a1


def attend_whole(s, v):
    m, l, a = attend(s, v)
    return a / l, m + jnp.log2(l)


def merge_whole(o0, z0, o1, z1):
    top, den, num = merge(z0, 1.0, o0, z1, 1.0, o1)
    return num / den, top + jnp.log2(den)


def split3(z, start=0, rest=0.0):
    hi = z.astype(BF16).astype(F32)
    mid = (z - hi).astype(BF16).astype(F32)
    lane = iota((z.shape[0], HD), 1) - start
    return jnp.where(
        lane == 0, hi, jnp.where(lane == 1, mid, jnp.where(lane == 2, z - hi - mid, rest)))


def join3(p, start=0):
    lane = iota(p.shape, 1) - start
    return jnp.sum(jnp.where((lane >= 0) & (lane < 3), p.astype(F32), 0.0), axis=1, keepdims=True)


def head(h):
    return slice(h * HD, (h + 1) * HD)


def head_copies(hbm, vmem, sems):
    def copy(n, h):
        return pltpu.make_async_copy(
            hbm[n].at[:, head(h)], vmem.at[n, :, head(h)], sems.at[n, h])

    for h in range(8):
        for n in range(3):
            copy(n, h).start()

    def arrive(h):
        for n in range(3):
            copy(n, h).wait()

    return arrive


def select_kernel(q, k, v, q1, kv1, x2, rows_in, wide, s1, s2, sems, sems_out):
    tp = lax.axis_index("tp")
    arrive = head_copies((q, k, v), rows_in, sems)
    pending = []

    def leave(src, dst, slot, h):
        copy = pltpu.make_async_copy(src, dst, sems_out.at[slot, h])
        copy.start()
        pending.append(copy)

    for h in range(8):
        arrive(h)
        far = []
        for n in range(3):
            buf = wide.at[(3 * h + n) % 6]
            buf[...] = rows_in[n, :, head(h)].astype(F32)
            s1[n, h] = buf[pl.ds(h % 4, 128, stride=4), :].astype(BF16)
            if n > 0:
                far.append(buf[pl.ds(8 * tp + h, 8, stride=64), :])
            s2[h, 32 * n : 32 * n + 32] = buf[pl.ds(8 * tp + h, 32, stride=16), :].astype(BF16)
        s2[h, 96:112] = jnp.concatenate(far, axis=0).astype(BF16)
        leave(s2.at[h], x2.at[h], 0, h)
        leave(s1.at[0, h], q1.at[h], 1, h)
        leave(s1.at[1, h], kv1.at[0, h], 2, h)
        leave(s1.at[2, h], kv1.at[1, h], 3, h)
    for copy in pending:
        copy.wait()


def local_kernel(qkv, keep, send, part, mine, theirs, rest, outs, tops, dens, sems_out):
    tp = lax.axis_index("tp")
    pending = []
    ok = iota((256, 256), 1) <= iota((256, 256), 0)
    for h in range(8):
        o_ref, m_ref, l_ref = outs.at[h % 4], tops.at[h % 4], dens.at[h % 4]
        for b in range(2):
            rows = slice(256 * b, 256 * b + 256)
            upto = slice(0, 256 * b + 256)
            s = dot_t(qkv[0, rows, head(h)], qkv[1, upto, head(h)]) * SCALE
            last = jnp.where(ok, s[:, 256 * b :], NEG)
            s = last if b == 0 else jnp.concatenate([s[:, :256], last], axis=1)
            m, l, a = attend(s, qkv[2, upto, head(h)])
            o_ref[rows, :] = a / l
            m_ref[rows, :] = jnp.broadcast_to(m, (256, HD))
            l_ref[rows, :] = jnp.broadcast_to(l, (256, HD))
        for n in range(3):
            r = (h + n + 1) % 4
            mine[h, n] = o_ref[pl.ds(r + 256 * tp, 64, stride=4), :].astype(BF16)
            theirs[h, n] = o_ref[pl.ds(r + 256 * (1 - tp), 64, stride=4), :].astype(BF16)
        pick = pl.ds(h % 4, 128, stride=4)
        rest[h, :, :HD] = o_ref[pick, :]
        rest[h, :, HD:] = m_ref[pick, :] + jnp.log2(l_ref[pick, :])
        for slot, (src, dst) in enumerate(((theirs, send), (mine, keep), (rest, part))):
            copy = pltpu.make_async_copy(src.at[h], dst.at[h], sems_out.at[slot, h])
            copy.start()
            pending.append(copy)
    for copy in pending:
        copy.wait()


def fetch_kernel(*refs):
    half = (len(refs) - 1) // 2
    sems = refs[-1]
    copies = []
    for n in range(half):
        for h in range(2):
            part = pl.ds(h * (refs[n].shape[0] // 2), refs[n].shape[0] // 2)
            copies.append(
                pltpu.make_async_copy(refs[n].at[part], refs[half + n].at[part], sems.at[n, h]))
    for copy in copies:
        copy.start()
    for copy in copies:
        copy.wait()


def near_kernel(q1, own, part, mate, far_a, far_b, keep, send, outs, tops, dens):
    tp = lax.axis_index("tp")
    c4 = lax.rem(lax.axis_index("ctx"), 4)
    row, col = iota((128, 512), 0), iota((128, 512), 1)
    start = jnp.where(c4 >= 2, 0, 256)
    stop = jnp.where(lax.rem(c4, 2) == 1, 384, 256)
    ok = ((col >= start) & (col < stop)) | ((col >= 384) & (col - 384 <= row))
    for h in range(8):
        keys = jnp.concatenate([far_a[0, h], far_b[0, h], mate[0, h], own[0, h]], axis=0)
        vals = jnp.concatenate([far_a[1, h], far_b[1, h], mate[1, h], own[1, h]], axis=0)
        m, l, a = attend(jnp.where(ok, dot_t(q1[h], keys) * SCALE, NEG), vals)
        outs[h] = a
        tops[h] = jnp.broadcast_to(m, (128, HD))
        dens[h] = jnp.broadcast_to(l, (128, HD))
    terms = [jnp.zeros((16, HD), F32)] * 2
    for h in range(8):
        top, den, num = merge(part[h, :, HD:], 1.0, part[h, :, :HD], tops[h], dens[h], outs[h])
        outs[h] = num / den
        tops[h] = top
        dens[h] = den
        for n, (ref, side) in enumerate(((keep, tp), (send, 1 - tp))):
            base = pl.multiple_of(64 * side, 64)
            ref[64 * h : 64 * h + 64] = outs[h, pl.ds(base, 64), :].astype(BF16)
            pick = pl.ds(64 * side + 2 * tp + h // 4, 16, stride=4)
            few = tops[h, pick, :] + jnp.log2(dens[h, pick, :])
            terms[n] = split3(few, 3 * h, terms[n])
    for ref, value in zip((keep, send), terms):
        ref[512:528] = value.astype(BF16)


def far_kernel(own, mate, line, g1, g2, g3, out, rows, sums, stats):
    c = lax.axis_index("ctx")
    x, y = lax.div(c, 32), lax.rem(lax.div(c, 8), 4)

    def part(ref, start):
        return ref[:, start : start + 32].astype(F32).reshape(256, HD)

    rows[...] = part(own, 0)
    keys = jnp.concatenate([part(mate, 0), part(own, 32)], axis=0).astype(BF16)
    vals = jnp.concatenate([part(mate, 32), part(own, 64)], axis=0).astype(BF16)
    s = dot_t(rows[...].astype(BF16), keys) * SCALE
    row, col = iota(s.shape, 0), iota(s.shape, 1)
    ok = ((col < 256) & (lax.rem(y, 2) == 1)) | ((col >= 256) & (col - 256 <= row))
    o2, z2 = attend_whole(jnp.where(ok, s, NEG), vals)
    sums[...] = o2
    stats[...] = jnp.broadcast_to(z2, (256, HD))

    q3 = rows[pl.ds(0, 64, stride=4), :].astype(BF16)
    keys, vals = [], []
    for ref in (g1, g2, g3, line):
        for j in range(4):
            b = ref[j].astype(F32)
            keys.append(b[:, 0:8].reshape(64, HD))
            vals.append(b[:, 8:16].reshape(64, HD))
    keys = jnp.concatenate(keys, axis=0).astype(BF16)
    vals = jnp.concatenate(vals, axis=0).astype(BF16)
    s = dot_t(q3, keys) * SCALE
    row, col = iota(s.shape, 0), iota(s.shape, 1)
    slot = lax.shift_right_logical(col, 6)
    earlier_x = (slot < 12) & (jnp.bitwise_xor(lax.shift_right_logical(slot, 2) + 1, x) < x)
    earlier_y = (slot > 12) & (jnp.bitwise_xor(slot - 12, y) < y)
    mine = (slot == 12) & (col - 768 <= row)
    o3, z3 = attend_whole(jnp.where(earlier_x | earlier_y | mine, s, NEG), vals)
    pick = pl.ds(0, 64, stride=4)
    o, z = merge_whole(sums[pick, :], stats[pick, :][:, 0:1], o3, z3)
    sums[pick, :] = o
    stats[pick, :] = jnp.broadcast_to(z, (64, HD))
    for j in range(16):
        out[j, :, :HD] = sums[16 * j : 16 * j + 16, :].astype(BF16)
        out[j, :, HD:] = split3(stats[16 * j : 16 * j + 16, :]).astype(BF16)


def join_kernel(ka, kb, ra, rb, back, out, wide):
    tp = lax.axis_index("tp")
    for h in range(8):
        for side, (first, second) in enumerate(((ka, kb), (ra, rb))):
            src = tp if side == 0 else 1 - tp
            buf = wide.at[(2 * h + side) % 4]
            for n in range(3):
                buf[pl.ds((h + n + 1) % 4, 64, stride=4), :] = first[h, n].astype(F32)
            buf[pl.ds(h % 4, 64, stride=4), :] = second[64 * h : 64 * h + 64].astype(F32)
            pick = pl.ds(8 * src + h, 16, stride=16)
            more = back[2 * h + src]
            _, den, num = merge(
                join3(second[512:528], 3 * h), 1.0, buf[pick, :],
                join3(more[:, HD:]), 1.0, more[:, :HD].astype(F32))
            buf[pick, :] = num / den
            cols = pl.ds(pl.multiple_of(src * 1024 + h * HD, HD), HD)
            out[:, cols] = buf[...].astype(BF16)


def call(kernel, ins, outs, scratch):
    vm, hbm = pl.BlockSpec(memory_space=VMEM), pl.BlockSpec(memory_space=pltpu.HBM)
    spaces = {"V": VMEM, "H": pltpu.HBM}
    args = [pltpu.with_memory_space_constraint(a, spaces[m]) if m else a for a, m in ins]
    return pl.pallas_call(
        kernel,
        out_shape=[spaces[m](*o) if m else jax.ShapeDtypeStruct(*o) for o, m in outs],
        in_specs=[hbm if m == "H" else vm for _, m in ins],
        out_specs=[hbm if m == "H" else vm for _, m in outs],
        scratch_shapes=scratch,
        compiler_params=pltpu.CompilerParams(vmem_limit_bytes=LIMIT),
    )(*args)


def local(queries, key_rows, value_rows):
    n = 128

    def exchange(value, axes, size, total):
        groups = [[size * b + i for i in range(size)] for b in range(total // size)]
        return lax.all_to_all(
            value, axes, split_axis=0, concat_axis=0, tiled=True, axis_index_groups=groups)

    def flip(value, bits):
        return lax.ppermute(value, "ctx", [(i, i ^ bits) for i in range(n)])

    barrier = lax.optimization_barrier
    dma = pltpu.SemaphoreType.DMA
    args = [(queries, "H"), (key_rows, "H"), (value_rows, "H")]
    q1, kv1, x2, rows = call(
        select_kernel, args,
        ((((8, 128, HD), BF16), "H"), (((2, 8, 128, HD), BF16), "H"), (((8, 112, HD), BF16), "H"),
         (((3, 512, 1024), BF16), "V")),
        [VMEM((6, 512, HD), F32), VMEM((3, 8, 128, HD), BF16),
         VMEM((8, 112, HD), BF16), dma((3, 8)), dma((4, 8))])
    y2 = exchange(x2, "ctx", 8, n)
    far_a = lax.ppermute(kv1, "ctx", [(i, i + 2) for i in range(n) if i % 4 < 2])
    mate = flip(kv1, 1)

    keep, send, part = call(
        local_kernel, [(rows, "V")],
        ((((8, 3, 64, HD), BF16), "H"), (((8, 3, 64, HD), BF16), "H"), (((8, 128, 256), F32), "H")),
        [VMEM((8, 3, 64, HD), BF16), VMEM((8, 3, 64, HD), BF16), VMEM((8, 128, 256), F32)]
        + [VMEM((4, 512, HD), F32)] * 3 + [dma((3, 8))])
    swap = [(0, 1), (1, 0)]
    y2, part = barrier((y2, part))
    kv2 = y2[:, 32:112]
    kv3 = y2[:, 96:112]
    flips = [flip(kv2 if j == 1 else kv3, 8 * j) for j in (1, 2, 3)]
    got = lax.ppermute(send, "tp", swap)

    line = jnp.stack([kv3, flips[0][:, 64:80], flips[1], flips[2]])
    ahead = [flip(line, 32 * j) for j in (1, 2, 3)]
    far_b = flip(far_a, 1)

    held = call(
        fetch_kernel, [(a, "H") for a in (q1, kv1, part)],
        [((a.shape, a.dtype), "V") for a in (q1, kv1, part)], [dma((3, 2))])
    keep1, send1 = call(
        near_kernel, [(a, "V") for a in (*held, mate, far_a, far_b)],
        ((((528, HD), BF16), None), (((528, HD), BF16), None)),
        [VMEM((8, 128, HD), F32)] * 3)
    got1 = lax.ppermute(send1, "tp", swap)

    y2, keep1 = barrier((y2, keep1))
    (back,) = call(
        far_kernel, [(a, "V") for a in (y2, flips[0], line, *ahead)],
        ((((16, 16, 256), BF16), None),), [VMEM((256, HD), F32)] * 3)
    back = exchange(back, ("ctx", "tp"), 16, 2 * n)

    (out,) = call(
        join_kernel, [(a, "V") for a in (keep, keep1, got, got1, back)],
        ((((256, 2048), BF16), None),), [VMEM((4, 256, HD), F32)])
    return out


def solution(mesh):
    return jax.shard_map(
        local,
        mesh=mesh,
        in_specs=(P("ctx", "tp"), P("ctx", "tp"), P("ctx", "tp")),
        out_specs=P(("ctx", "tp"), None),
        check_vma=False,
    )
```

```python
import functools
import math

import jax
import jax.numpy as jnp
from jax import lax
from jax.experimental import pallas as pl
from jax.experimental.pallas import tpu as pltpu
from jax.sharding import PartitionSpec as P


F32 = jnp.float32
BF16 = jnp.bfloat16
HD = 128
NEG = -1e30
SCALE = math.log2(math.e) / math.sqrt(HD)
VMEM = pltpu.VMEM
LIMIT = 24 * 2**20


def dot_t(a, b):
    return lax.dot_general(a, b, (((1,), (1,)), ((), ())), preferred_element_type=F32)


def dot(a, b):
    return lax.dot_general(a, b, (((1,), (0,)), ((), ())), preferred_element_type=F32)


def iota(shape, axis):
    return lax.broadcasted_iota(jnp.int32, shape, axis)


def attend(s, v):
    m = jnp.max(s, axis=1, keepdims=True)
    e = jnp.exp2(s - m)
    return m, jnp.sum(e, axis=1, keepdims=True), dot(e.astype(BF16), v)


def merge(m0, l0, a0, m1, l1, a1):
    top = jnp.maximum(m0, m1)
    w0, w1 = jnp.exp2(m0 - top), jnp.exp2(m1 - top)
    return top, w0 * l0 + w1 * l1, w0 * a0 + w1 * a1


def attend_whole(s, v):
    m, l, a = attend(s, v)
    return a / l, m + jnp.log2(l)


def merge_whole(o0, z0, o1, z1):
    top, den, num = merge(z0, 1.0, o0, z1, 1.0, o1)
    return num / den, top + jnp.log2(den)


def split3(z, start=0, rest=0.0):
    hi = z.astype(BF16).astype(F32)
    mid = (z - hi).astype(BF16).astype(F32)
    lane = iota((z.shape[0], HD), 1) - start
    return jnp.where(
        lane == 0, hi, jnp.where(lane == 1, mid, jnp.where(lane == 2, z - hi - mid, rest)))


def join3(p, start=0):
    lane = iota(p.shape, 1) - start
    return jnp.sum(jnp.where((lane >= 0) & (lane < 3), p.astype(F32), 0.0), axis=1, keepdims=True)


def head(h):
    return slice(h * HD, (h + 1) * HD)


def head_copies(hbm, vmem, sems):
    def copy(n, h):
        return pltpu.make_async_copy(
            hbm[n].at[:, head(h)], vmem.at[n, :, head(h)], sems.at[n, h])

    for h in range(8):
        for n in range(3):
            copy(n, h).start()

    def arrive(h):
        for n in range(3):
            copy(n, h).wait()

    return arrive


def select_kernel(q, k, v, q1, kv1, x2, rows_in, wide, s1, s2, sems, sems_out):
    tp = lax.axis_index("tp")
    arrive = head_copies((q, k, v), rows_in, sems)
    pending = []

    def leave(src, dst, slot, h):
        copy = pltpu.make_async_copy(src, dst, sems_out.at[slot, h])
        copy.start()
        pending.append(copy)

    for h in range(8):
        arrive(h)
        far = []
        for n in range(3):
            buf = wide.at[(3 * h + n) % 6]
            buf[...] = rows_in[n, :, head(h)].astype(F32)
            s1[n, h] = buf[pl.ds(h % 4, 128, stride=4), :].astype(BF16)
            if n > 0:
                far.append(buf[pl.ds(8 * tp + h, 8, stride=64), :])
            s2[h, 32 * n : 32 * n + 32] = buf[pl.ds(8 * tp + h, 32, stride=16), :].astype(BF16)
        s2[h, 96:112] = jnp.concatenate(far, axis=0).astype(BF16)
        leave(s2.at[h], x2.at[h], 0, h)
        leave(s1.at[0, h], q1.at[h], 1, h)
        leave(s1.at[1, h], kv1.at[0, h], 2, h)
        leave(s1.at[2, h], kv1.at[1, h], 3, h)
    for copy in pending:
        copy.wait()


def local_kernel(heads, qkv, *refs):
    keep, send, part, mine, theirs, rest, outs, tops, dens, sems_out = refs[-10:]
    tp = lax.axis_index("tp")
    pending = []
    ok = iota((256, 256), 1) <= iota((256, 256), 0)
    for h in heads:
        o_ref, m_ref, l_ref = outs.at[h % 4], tops.at[h % 4], dens.at[h % 4]
        for b in range(2):
            rows = slice(256 * b, 256 * b + 256)
            upto = slice(0, 256 * b + 256)
            s = dot_t(qkv[0, rows, head(h)], qkv[1, upto, head(h)]) * SCALE
            last = jnp.where(ok, s[:, 256 * b :], NEG)
            s = last if b == 0 else jnp.concatenate([s[:, :256], last], axis=1)
            m, l, a = attend(s, qkv[2, upto, head(h)])
            o_ref[rows, :] = a / l
            m_ref[rows, :] = jnp.broadcast_to(m, (256, HD))
            l_ref[rows, :] = jnp.broadcast_to(l, (256, HD))
        for n in range(3):
            r = (h + n + 1) % 4
            mine[h, n] = o_ref[pl.ds(r + 256 * tp, 64, stride=4), :].astype(BF16)
            theirs[h, n] = o_ref[pl.ds(r + 256 * (1 - tp), 64, stride=4), :].astype(BF16)
        pick = pl.ds(h % 4, 128, stride=4)
        rest[h, :, :HD] = o_ref[pick, :]
        rest[h, :, HD:] = m_ref[pick, :] + jnp.log2(l_ref[pick, :])
        for slot, (src, dst) in enumerate(((theirs, send), (mine, keep), (rest, part))):
            copy = pltpu.make_async_copy(src.at[h], dst.at[h], sems_out.at[slot, h])
            copy.start()
            pending.append(copy)
    for copy in pending:
        copy.wait()


def fetch_kernel(*refs):
    half = (len(refs) - 1) // 2
    sems = refs[-1]
    copies = []
    for n in range(half):
        for h in range(2):
            part = pl.ds(h * (refs[n].shape[0] // 2), refs[n].shape[0] // 2)
            copies.append(
                pltpu.make_async_copy(refs[n].at[part], refs[half + n].at[part], sems.at[n, h]))
    for copy in copies:
        copy.start()
    for copy in copies:
        copy.wait()


def near_kernel(q1, own, part, mate, far_a, far_b, keep, send, outs, tops, dens):
    tp = lax.axis_index("tp")
    c4 = lax.rem(lax.axis_index("ctx"), 4)
    row, col = iota((128, 512), 0), iota((128, 512), 1)
    start = jnp.where(c4 >= 2, 0, 256)
    stop = jnp.where(lax.rem(c4, 2) == 1, 384, 256)
    ok = ((col >= start) & (col < stop)) | ((col >= 384) & (col - 384 <= row))
    for h in range(8):
        keys = jnp.concatenate([far_a[0, h], far_b[0, h], mate[0, h], own[0, h]], axis=0)
        vals = jnp.concatenate([far_a[1, h], far_b[1, h], mate[1, h], own[1, h]], axis=0)
        m, l, a = attend(jnp.where(ok, dot_t(q1[h], keys) * SCALE, NEG), vals)
        outs[h] = a
        tops[h] = jnp.broadcast_to(m, (128, HD))
        dens[h] = jnp.broadcast_to(l, (128, HD))
    terms = [jnp.zeros((16, HD), F32)] * 2
    for h in range(8):
        top, den, num = merge(part[h, :, HD:], 1.0, part[h, :, :HD], tops[h], dens[h], outs[h])
        outs[h] = num / den
        tops[h] = top
        dens[h] = den
        for n, (ref, side) in enumerate(((keep, tp), (send, 1 - tp))):
            base = pl.multiple_of(64 * side, 64)
            ref[64 * h : 64 * h + 64] = outs[h, pl.ds(base, 64), :].astype(BF16)
            pick = pl.ds(64 * side + 2 * tp + h // 4, 16, stride=4)
            few = tops[h, pick, :] + jnp.log2(dens[h, pick, :])
            terms[n] = split3(few, 3 * h, terms[n])
    for ref, value in zip((keep, send), terms):
        ref[512:528] = value.astype(BF16)


def far_kernel(own, mate, line, g1, g2, g3, out, rows, sums, stats):
    c = lax.axis_index("ctx")
    x, y = lax.div(c, 32), lax.rem(lax.div(c, 8), 4)

    def part(ref, start):
        return ref[:, start : start + 32].astype(F32).reshape(256, HD)

    rows[...] = part(own, 0)
    keys = jnp.concatenate([part(mate, 0), part(own, 32)], axis=0).astype(BF16)
    vals = jnp.concatenate([part(mate, 32), part(own, 64)], axis=0).astype(BF16)
    s = dot_t(rows[...].astype(BF16), keys) * SCALE
    row, col = iota(s.shape, 0), iota(s.shape, 1)
    ok = ((col < 256) & (lax.rem(y, 2) == 1)) | ((col >= 256) & (col - 256 <= row))
    o2, z2 = attend_whole(jnp.where(ok, s, NEG), vals)
    sums[...] = o2
    stats[...] = jnp.broadcast_to(z2, (256, HD))

    q3 = rows[pl.ds(0, 64, stride=4), :].astype(BF16)
    keys, vals = [], []
    for ref in (g1, g2, g3, line):
        for j in range(4):
            b = ref[j].astype(F32)
            keys.append(b[:, 0:8].reshape(64, HD))
            vals.append(b[:, 8:16].reshape(64, HD))
    keys = jnp.concatenate(keys, axis=0).astype(BF16)
    vals = jnp.concatenate(vals, axis=0).astype(BF16)
    s = dot_t(q3, keys) * SCALE
    row, col = iota(s.shape, 0), iota(s.shape, 1)
    slot = lax.shift_right_logical(col, 6)
    earlier_x = (slot < 12) & (jnp.bitwise_xor(lax.shift_right_logical(slot, 2) + 1, x) < x)
    earlier_y = (slot > 12) & (jnp.bitwise_xor(slot - 12, y) < y)
    mine = (slot == 12) & (col - 768 <= row)
    o3, z3 = attend_whole(jnp.where(earlier_x | earlier_y | mine, s, NEG), vals)
    pick = pl.ds(0, 64, stride=4)
    o, z = merge_whole(sums[pick, :], stats[pick, :][:, 0:1], o3, z3)
    sums[pick, :] = o
    stats[pick, :] = jnp.broadcast_to(z, (64, HD))
    for j in range(16):
        out[j, :, :HD] = sums[16 * j : 16 * j + 16, :].astype(BF16)
        out[j, :, HD:] = split3(stats[16 * j : 16 * j + 16, :]).astype(BF16)


def join_kernel(ka, kb, ra, rb, back, out, wide):
    tp = lax.axis_index("tp")
    for h in range(8):
        for side, (first, second) in enumerate(((ka, kb), (ra, rb))):
            src = tp if side == 0 else 1 - tp
            buf = wide.at[(2 * h + side) % 4]
            for n in range(3):
                buf[pl.ds((h + n + 1) % 4, 64, stride=4), :] = first[h, n].astype(F32)
            buf[pl.ds(h % 4, 64, stride=4), :] = second[64 * h : 64 * h + 64].astype(F32)
            pick = pl.ds(8 * src + h, 16, stride=16)
            more = back[2 * h + src]
            _, den, num = merge(
                join3(second[512:528], 3 * h), 1.0, buf[pick, :],
                join3(more[:, HD:]), 1.0, more[:, :HD].astype(F32))
            buf[pick, :] = num / den
            cols = pl.ds(pl.multiple_of(src * 1024 + h * HD, HD), HD)
            out[:, cols] = buf[...].astype(BF16)


def call(kernel, ins, outs, scratch, aliases={}):
    vm, hbm = pl.BlockSpec(memory_space=VMEM), pl.BlockSpec(memory_space=pltpu.HBM)
    spaces = {"V": VMEM, "H": pltpu.HBM}
    args = [pltpu.with_memory_space_constraint(a, spaces[m]) if m else a for a, m in ins]
    return pl.pallas_call(
        kernel,
        out_shape=[spaces[m](*o) if m else jax.ShapeDtypeStruct(*o) for o, m in outs],
        in_specs=[hbm if m == "H" else vm for _, m in ins],
        out_specs=[hbm if m == "H" else vm for _, m in outs],
        scratch_shapes=scratch,
        compiler_params=pltpu.CompilerParams(
            vmem_limit_bytes=LIMIT),
        input_output_aliases=aliases,
    )(*args)


def local(queries, key_rows, value_rows):
    n = 128

    def exchange(value, axes, size, total):
        groups = [[size * b + i for i in range(size)] for b in range(total // size)]
        return lax.all_to_all(
            value, axes, split_axis=0, concat_axis=0, tiled=True, axis_index_groups=groups)

    def flip(value, bits):
        return lax.ppermute(value, "ctx", [(i, i ^ bits) for i in range(n)])

    barrier = lax.optimization_barrier
    dma = pltpu.SemaphoreType.DMA
    args = [(queries, "H"), (key_rows, "H"), (value_rows, "H")]
    q1, kv1, x2, rows = call(
        select_kernel, args,
        ((((8, 128, HD), BF16), "H"), (((2, 8, 128, HD), BF16), "H"), (((8, 112, HD), BF16), "H"),
         (((3, 512, 1024), BF16), "V")),
        [VMEM((6, 512, HD), F32), VMEM((3, 8, 128, HD), BF16),
         VMEM((8, 112, HD), BF16), dma((3, 8)), dma((4, 8))])
    y2 = exchange(x2, "ctx", 8, n)
    far_a = lax.ppermute(kv1, "ctx", [(i, i + 2) for i in range(n) if i % 4 < 2])
    mate = flip(kv1, 1)

    def attend_local(heads, before=()):
        return call(
            functools.partial(local_kernel, heads), [(rows, "V")] + [(a, "H") for a in before],
            ((((8, 3, 64, HD), BF16), "H"), (((8, 3, 64, HD), BF16), "H"),
             (((8, 128, 256), F32), "H")),
            [VMEM((8, 3, 64, HD), BF16), VMEM((8, 3, 64, HD), BF16), VMEM((8, 128, 256), F32)]
            + [VMEM((4, 512, HD), F32)] * 3 + [dma((3, 8))],
            {1: 0, 2: 1, 3: 2} if before else {})

    keep, send, part = attend_local(range(6))
    swap = [(0, 1), (1, 0)]
    y2, part = barrier((y2, part))
    kv2 = y2[:, 32:112]
    kv3 = y2[:, 96:112]
    flips = [flip(kv2 if j == 1 else kv3, 8 * j) for j in (1, 2, 3)]
    keep, send, part = attend_local(range(6, 8), (keep, send, part))
    got = lax.ppermute(send, "tp", swap)

    line = jnp.stack([kv3, flips[0][:, 64:80], flips[1], flips[2]])
    ahead = [flip(line, 32 * j) for j in (1, 2, 3)]
    far_b = flip(far_a, 1)

    held = call(
        fetch_kernel, [(a, "H") for a in (q1, kv1, part)],
        [((a.shape, a.dtype), "V") for a in (q1, kv1, part)], [dma((3, 2))])
    keep1, send1 = call(
        near_kernel, [(a, "V") for a in (*held, mate, far_a, far_b)],
        ((((528, HD), BF16), None), (((528, HD), BF16), None)),
        [VMEM((8, 128, HD), F32)] * 3)
    got1 = lax.ppermute(send1, "tp", swap)

    y2, keep1 = barrier((y2, keep1))
    (back,) = call(
        far_kernel, [(a, "V") for a in (y2, flips[0], line, *ahead)],
        ((((16, 16, 256), BF16), None),), [VMEM((256, HD), F32)] * 3)
    back = exchange(back, ("ctx", "tp"), 16, 2 * n)

    (out,) = call(
        join_kernel, [(a, "V") for a in (keep, keep1, got, got1, back)],
        ((((256, 2048), BF16), None),), [VMEM((4, 256, HD), F32)])
    return out


def solution(mesh):
    return jax.shard_map(
        local,
        mesh=mesh,
        in_specs=(P("ctx", "tp"), P("ctx", "tp"), P("ctx", "tp")),
        out_specs=P(("ctx", "tp"), None),
        check_vma=False,
    )
```
